512 devices in a mesh: row: 32 (over z_hi, y, core), col: 16 (over z_lo, x).
Axes of the slice: x: 4, y: 8, z: 8 (z_hi: 2, z_lo: 4; z = z_hi * 4 + z_lo), core: 2. Of those that a mesh axis runs over, the one named last changes fastest.
Arguments:
- sources: float32 [32, 16, 512, 512], P('row', 'col'), may hold values from -6 to 6
- leaf_basis: float32 [32, 16, 512, 256], P('row', 'col'), may hold values from -0.25 to 0.25
- transfers: float32 [32, 16, 4, 256, 512], P('row', 'col'), may hold values from -0.25 to 0.25
- out_basis: float32 [32, 16, 512, 256], P('row', 'col'), may hold values from -0.375 to 0.375
Outputs:
- result: float32 [32, 16, 512, 512], P('row', 'col')
The draws below stay inside these ranges and needn't reach their ends.
All inputs are finite; a program needn't handle non-finite values.
Results may differ from the reference program's by a relative error of at most 0.0001.
Values sent between devices are 32-bit elements; how exact they have to be, the bound alone decides.
No kernel may reach another device: no remote copies, remote signals or barrier semaphores. Data moves between devices by JAX's collectives and lax.ppermute only.
A program may use at most 64 MiB of HBM per device.

```python
import jax
import jax.numpy as jnp
from jax import lax

LEAF = 512
RANK = 256
RHS = 512
LEVELS = 4
N_ROW = 32
N_COL = 16


def levels(rng, dims, cuts, least, high):
    factor_of = 1.0
    for axis_at, blocks in cuts:
        draws = jax.random.uniform(jax.random.fold_in(jax.random.fold_in(rng, 6), axis_at), (blocks,), jnp.float32, least / len(cuts), high / len(cuts))
        factor_of = factor_of * jnp.repeat(jnp.exp(draws), dims[axis_at] // blocks).reshape((-1,) + (1,) * (len(dims) - 1 - axis_at))
    return factor_of


def gaussian(key, dims, deviation, limit, shards=(), held_as=jnp.bfloat16):
    drawn = deviation * jax.random.normal(key, dims, jnp.float32)
    if shards:
        drawn = drawn * levels(key, dims, shards, -0.22, 0.18)
    return jnp.clip(drawn, -limit, limit).astype(held_as)


def setup_inputs(seed: int = 0) -> dict:
    seeds = jax.random.split(jax.random.key(seed), 5)
    sources = gaussian(seeds[0], (N_ROW, N_COL, LEAF, RHS), 1.0, 6.0, ((0, 32), (1, 16)), jnp.float32)
    leaf_basis = gaussian(seeds[1], (N_ROW, N_COL, LEAF, RANK), LEAF ** -0.5, 0.25, ((0, 32), (1, 16)), jnp.float32)
    transfers = gaussian(seeds[2], (N_ROW, N_COL, LEVELS, RANK, 2 * RANK), (2 * RANK) ** -0.5, 0.25, ((0, 32), (1, 16)), jnp.float32)
    out_basis = gaussian(seeds[3], (N_ROW, N_COL, LEAF, RANK), RANK ** -0.5, 0.375, ((0, 32), (1, 16)), jnp.float32)
    return {"sources": sources, "leaf_basis": leaf_basis, "transfers": transfers, "out_basis": out_basis}


def partner(coeff, axis, bit):
    span = 1 << bit
    shape = coeff.shape
    if axis == 0:
        split = coeff.reshape((shape[0] // (2 * span), 2, span) + shape[1:])
        return jnp.flip(split, 1).reshape(shape)
    split = coeff.reshape((shape[0], shape[1] // (2 * span), 2, span) + shape[2:])
    return jnp.flip(split, 2).reshape(shape)


def reference(sources, leaf_basis, transfers, out_basis):
    high = lax.Precision.HIGHEST
    coeff = jnp.einsum("abmk,abmr->abkr", leaf_basis, sources, precision=high)
    row_bits = N_ROW.bit_length() - 1
    col_bits = N_COL.bit_length() - 1
    for level in range(LEVELS):
        if level % 2 == 0:
            other = partner(coeff, 0, row_bits - 1 - level // 2)
        else:
            other = partner(coeff, 1, col_bits - 1 - level // 2)
        block = transfers[:, :, level]
        coeff = jnp.einsum("abkj,abjr->abkr", block[..., :RANK], coeff, precision=high) + jnp.einsum("abkj,abjr->abkr", block[..., RANK:], other, precision=high)
    return jnp.einsum("abmk,abkr->abmr", out_basis, coeff, precision=high)
```

```python
import jax
import jax.numpy as jnp
from jax import lax
from jax.experimental.layout import Layout, with_layout_constraint
from jax.sharding import PartitionSpec as P

STEPS = [(0, 0, 1), (0, 1, 2), (0, 2, 3), (0, 3, 4), (1, 0, 1), (1, 1, 2), (1, 2, 3), (1, 3, 4), (2, 0, 1), (2, 1, 2), (2, 2, 3), (2, 3, 4), (3, 0, 1), (3, 1, 2), (3, 2, 3), (3, 3, 4), (4, 0, 1), (4, 1, 2), (4, 2, 3), (4, 3, 4)]
PARTS = 4
HIGH = lax.Precision.HIGH


def swapped(x, axis, apart):
    return lax.ppermute(x, axis, [(i, i ^ 1 << apart) for i in range(lax.axis_size(axis))])


def dot(a, b):
    return jnp.dot(a, b, precision=HIGH, preferred_element_type=jnp.float32)


def pinned(x):
    return with_layout_constraint(x, Layout((0, 1)))


def body(sources, leaf_basis, transfers, out_basis):
    levels = transfers.shape[2]
    rank, width = leaf_basis.shape[3], sources.shape[3] // PARTS
    row_bits = lax.axis_size("row").bit_length() - 1
    col_bits = lax.axis_size("col").bit_length() - 1

    def partner(x, level):
        if level % 2 == 0:
            return swapped(x, "row", row_bits - 1 - level // 2)
        return swapped(x, "col", col_bits - 1 - level // 2)

    coeff = jnp.einsum("mk,mr->kr", leaf_basis[0, 0], sources[0, 0], precision=HIGH, preferred_element_type=jnp.float32)
    sent = [[] for _ in range(levels)]
    out, token = [], None
    for level, lo, hi in STEPS:
        if level == 0:
            now = coeff[:, lo * width:hi * width]
            if token is not None:
                now, token = lax.optimization_barrier((now, token))
        else:
            pieces = []
            for a, b, own, other in sent[level - 1]:
                x, y = max(a, lo), min(b, hi)
                if x < y:
                    cut = slice((x - a) * width, (y - a) * width)
                    kept, token = lax.optimization_barrier((own[:, cut], token))
                    pieces.append(kept + dot(transfers[0, 0, level - 1][:, rank:], other[:, cut]))
            now = pinned(jnp.concatenate(pieces, axis=1) if len(pieces) > 1 else pieces[0])
        if level < levels:
            own = dot(transfers[0, 0, level][:, :rank], now)
            sent[level].append((lo, hi, own, partner(now, level)))
            token = own
        else:
            token = pinned(dot(out_basis[0, 0], now))
            out.append((lo, token))
    out = [x for _, x in sorted(out, key=lambda e: e[0])]
    result = jnp.concatenate(out, axis=1) if len(out) > 1 else out[0]
    return result[None, None]


def solution(mesh):
    in_specs = (
        P("row", "col", None, None),
        P("row", "col", None, None),
        P("row", "col", None, None, None),
        P("row", "col", None, None),
    )
    out_specs = P("row", "col", None, None)
    return jax.shard_map(body, mesh=mesh, in_specs=in_specs, out_specs=out_specs, check_vma=False)
```

```python
import jax
import jax.numpy as jnp
from jax import lax
from jax.experimental.layout import Layout, with_layout_constraint
from jax.sharding import PartitionSpec as P

STEPS = [(0, 0, 1), (0, 1, 2), (0, 2, 3), (0, 3, 4), (1, 0, 1), (1, 1, 2), (1, 2, 3), (1, 3, 4), (2, 0, 1), (2, 1, 2), (2, 2, 3), (2, 3, 4), (3, 0, 1), (3, 1, 2), (3, 2, 3), (3, 3, 4), (4, 0, 1), (4, 1, 2), (4, 2, 3), (4, 3, 4)]
PARTS = 4
HIGH = lax.Precision.HIGH


def swapped(x, axis, apart):
    return lax.ppermute(x, axis, [(i, i ^ 1 << apart) for i in range(lax.axis_size(axis))])


def dot(a, b):
    return jnp.dot(a, b, precision=HIGH, preferred_element_type=jnp.float32)


def pinned(x):
    return with_layout_constraint(x, Layout((0, 1)))


def body(sources, leaf_basis, transfers, out_basis):
    levels = transfers.shape[2]
    rank, width = leaf_basis.shape[3], sources.shape[3] // PARTS
    row_bits = lax.axis_size("row").bit_length() - 1
    col_bits = lax.axis_size("col").bit_length() - 1

    def partner(x, level):
        if level % 2 == 0:
            return swapped(x, "row", row_bits - 1 - level // 2)
        return swapped(x, "col", col_bits - 1 - level // 2)

    coeff = jnp.einsum("mk,mr->kr", leaf_basis[0, 0], sources[0, 0], precision=HIGH, preferred_element_type=jnp.float32)
    sent = [[] for _ in range(levels)]
    out, token = [], None
    for level, lo, hi in STEPS:
        if level == 0:
            now = coeff[:, lo * width:hi * width]
            if token is not None:
                now, token = lax.optimization_barrier((now, token))
        else:
            pieces = []
            for a, b, own, other in sent[level - 1]:
                x, y = max(a, lo), min(b, hi)
                if x < y:
                    cut = slice((x - a) * width, (y - a) * width)
                    kept, token = lax.optimization_barrier((own[:, cut], token))
                    pieces.append(kept + dot(transfers[0, 0, level - 1][:, rank:], other[:, cut]))
            now = pinned(jnp.concatenate(pieces, axis=1) if len(pieces) > 1 else pieces[0])
        if level < levels:
            own = dot(transfers[0, 0, level][:, :rank], now)
            sent[level].append((lo, hi, own, partner(now, level)))
            token = own
        else:
            token = pinned(dot(out_basis[0, 0], now))
            out.append((lo, token))
    out = sorted(out, key=lambda e: e[0])
    early = [x for _, x in out[:-1]] + [jnp.zeros_like(out[-1][1])]
    result = lax.dynamic_update_slice(jnp.concatenate(early, axis=1), out[-1][1], (0, out[-1][0] * width))
    return result[None, None]


def solution(mesh):
    in_specs = (
        P("row", "col", None, None),
        P("row", "col", None, None),
        P("row", "col", None, None, None),
        P("row", "col", None, None),
    )
    out_specs = P("row", "col", None, None)
    return jax.shard_map(body, mesh=mesh, in_specs=in_specs, out_specs=out_specs, check_vma=False)
```

```python
import jax
import jax.numpy as jnp
from jax import lax
from jax.experimental.layout import Layout, with_layout_constraint
from jax.sharding import PartitionSpec as P

STEPS = [(0, 0, 1), (0, 1, 2), (0, 2, 3), (0, 3, 4), (1, 0, 1), (1, 1, 2), (1, 2, 3), (1, 3, 4), (2, 0, 1), (2, 1, 2), (2, 2, 3), (2, 3, 4), (3, 0, 1), (3, 1, 2), (3, 2, 3), (3, 3, 4), (4, 0, 1), (4, 1, 2), (4, 2, 3), (4, 3, 4)]
PARTS = 4
HIGH = lax.Precision.HIGH


def swapped(x, axis, apart):
    return lax.ppermute(x, axis, [(i, i ^ 1 << apart) for i in range(lax.axis_size(axis))])


def dot(a, b):
    return jnp.dot(a, b, precision=HIGH, preferred_element_type=jnp.float32)


def pinned(x):
    return with_layout_constraint(x, Layout((0, 1)))


def body(sources, leaf_basis, transfers, out_basis):
    levels = transfers.shape[2]
    rank, width = leaf_basis.shape[3], sources.shape[3] // PARTS
    row_bits = lax.axis_size("row").bit_length() - 1
    col_bits = lax.axis_size("col").bit_length() - 1

    def partner(x, level):
        if level % 2 == 0:
            return swapped(x, "row", row_bits - 1 - level // 2)
        return swapped(x, "col", col_bits - 1 - level // 2)

    coeff = jnp.einsum("mk,mr->kr", leaf_basis[0, 0], sources[0, 0], precision=HIGH, preferred_element_type=jnp.float32)
    every = dot(transfers[0, 0, 0][:, :rank], coeff)
    sent = [[] for _ in range(levels)]
    out, token = [], None
    for level, lo, hi in STEPS:
        if level == 0:
            now = coeff[:, lo * width:hi * width]
        else:
            pieces = []
            for a, b, own, other in sent[level - 1]:
                x, y = max(a, lo), min(b, hi)
                if x < y:
                    cut = slice((x - a) * width, (y - a) * width)
                    kept, token = lax.optimization_barrier((own[:, cut], token))
                    pieces.append(kept + dot(transfers[0, 0, level - 1][:, rank:], other[:, cut]))
            now = pinned(jnp.concatenate(pieces, axis=1) if len(pieces) > 1 else pieces[0])
        if level < levels:
            own = every[:, lo * width:hi * width] if level == 0 else dot(transfers[0, 0, level][:, :rank], now)
            sent[level].append((lo, hi, own, partner(now, level)))
            token = every if level == 0 else own
        else:
            token = pinned(dot(out_basis[0, 0], now))
            out.append((lo, token))
    out = sorted(out, key=lambda e: e[0])
    early = [x for _, x in out[:-1]] + [jnp.zeros_like(out[-1][1])]
    result = lax.dynamic_update_slice(jnp.concatenate(early, axis=1), out[-1][1], (0, out[-1][0] * width))
    return result[None, None]


def solution(mesh):
    in_specs = (
        P("row", "col", None, None),
        P("row", "col", None, None),
        P("row", "col", None, None, None),
        P("row", "col", None, None),
    )
    out_specs = P("row", "col", None, None)
    return jax.shard_map(body, mesh=mesh, in_specs=in_specs, out_specs=out_specs, check_vma=False)
```
